32 devices in a mesh: row: 8 (over y, x, core), col: 4 (over z).
Axes of the slice: x: 2, y: 2, z: 4, core: 2. Of those that a mesh axis runs over, the one named last changes fastest.
Arguments:
- pixels: float32 [8, 3, 1024, 2048], P(None, None, 'row', 'col'), may hold values from -6 to 6
- factor: float32 [1024, 512], P('row'), may hold values from -6 to 6
Outputs:
- gram: float32 [1024, 1024], P('row', 'col')
- projected: float32 [1024, 512], P('col', 'row')
The draws below stay inside these ranges and needn't reach their ends.
All inputs are finite; a program needn't handle non-finite values.
Results may differ from the reference program's by a relative error of at most 0.000075.
Values sent between devices are 32-bit elements; how exact they have to be, the bound alone decides.
A program may use at most 64 MiB of HBM per device.

```python
import jax
import jax.numpy as jnp
from jax import lax

H = 1024
W = 2048
C = 3
R = 512
VIEWS = 8


def levels(stream_key, dims, pieces, low, top_value):
    gain, own = 1.0, jax.random.fold_in(stream_key, 6)
    for axis_at, blocks in pieces:
        heights = jnp.exp(jax.random.uniform(jax.random.fold_in(own, axis_at), (blocks,), jnp.float32, low / len(pieces), top_value / len(pieces)))
        gain = gain * jnp.repeat(heights, dims[axis_at] // blocks).reshape([-1 if axis == axis_at else 1 for axis in range(len(dims))])
    return gain


def noise(rng, dims, spread, most, shards=(), kind=jnp.bfloat16):
    values = jax.random.normal(rng, dims, jnp.float32) * spread
    if len(shards) > 0:
        values = levels(rng, dims, shards, -0.22, 0.18) * values
    return jnp.clip(values, min=-most, max=most).astype(kind)


def setup_inputs(seed: int = 0) -> dict:
    streams_of = jax.random.split(jax.random.key(seed), 3)
    pixels = noise(streams_of[0], (VIEWS, C, H, W), 1.0, 6.0, ((2, 8), (3, 4)), jnp.float32)
    factor = noise(streams_of[1], (H, R), 1.0, 6.0, ((0, 8),), jnp.float32)
    return {"pixels": pixels, "factor": factor}


def reference(pixels, factor):
    unfolded = jnp.transpose(pixels, (2, 0, 1, 3)).reshape(H, VIEWS * C * W)
    gram = jnp.dot(unfolded, unfolded.T, precision=lax.Precision.HIGHEST, preferred_element_type=jnp.float32)
    gram = gram / jnp.float32(VIEWS * C * W)
    projected = jnp.dot(gram.T, factor, precision=lax.Precision.HIGHEST, preferred_element_type=jnp.float32)
    return gram, projected
```

```python
import functools

import jax
import jax.numpy as jnp
from jax import lax
from jax.experimental import pallas as pl
from jax.experimental.pallas import tpu as pltpu
from jax.sharding import PartitionSpec as P

MESH = pl.DeviceIdType.MESH

EARLY = {(0, 0): (0, 0), (1, 0): (3, 0), (1, 1): (1, 0), (2, 0): (3, 1), (2, 1): (0, 1), (2, 2): (2, 0)}
PAIRS = list(EARLY)
SLOTS = 2


def flip(value, mask, bits):
    out = 0
    for b in range(bits):
        bit = (value // (1 << b)) % 2
        out = out + (1 << b) * ((1 - bit) if (mask >> b) & 1 else bit)
    return out


def differ(left, right, bits):
    out = 0
    for b in range(bits):
        out = out + (1 << b) * (((left // (1 << b)) + (right // (1 << b))) % 2)
    return out


def dot_t(a, b):
    return lax.dot_general(a, b, (((1,), (1,)), ((), ())), preferred_element_type=jnp.float32)


def kernel(
    rows, cols, scale, cuts,
    pix, fac, gram, proj,
    xs, hi, lo, part, pair_in, summed, z_in, esum, ed_in, em_in,
    lpart, lpair, lsum, lz_in, lout, ld_in, lm_in, work, term, term_in,
    own_sem, a_send, a_recv, d_send, d_recv, p_send, p_recv, z_send, z_recv, e_send, e_recv, em_send, em_recv,
    lp_send, lp_recv, lz_send, lz_recv, ld_send, ld_recv, lm_send, lm_recv, t_send, t_recv,
):
    r = lax.axis_index("row")
    z = lax.axis_index("col")
    core = r % 2
    chip = r // 2
    rbits = rows.bit_length() - 1
    zbits = cols.bit_length() - 1
    chips = rows // 2
    far = chips - 1
    mine = differ(chip, z, zbits)
    per = pix.shape[0] // rows
    block = pix.shape[1]
    depth = pix.shape[2]
    mate = [flip(r, k, rbits) for k in range(rows)]
    zs = [flip(z, k, zbits) for k in range(cols)]
    near = [flip(chip, i, zbits) for i in range(chips)]
    strips = list(zip(cuts[:-1], cuts[1:]))

    def remote(src, dst, send, recv, row, plane):
        return pltpu.make_async_remote_copy(
            src_ref=src, dst_ref=dst, send_sem=send, recv_sem=recv, device_id=(row, plane), device_id_type=MESH
        )

    barrier = pltpu.get_barrier_semaphore()
    for k in range(rows):
        for kz in range(cols):
            if k or kz:
                pl.semaphore_signal(barrier, inc=1, device_id=(mate[k], zs[kz]), device_id_type=MESH)
    own = pltpu.make_async_copy(pix.at[pl.ds(r * per, per)], xs.at[0], own_sem)
    own.start()
    hi[far] = jnp.zeros(hi.shape[1:], hi.dtype)
    lo[far] = jnp.zeros(lo.shape[1:], lo.dtype)
    pl.semaphore_wait(barrier, rows * cols - 1)

    def whole(k):
        return remote(pix.at[pl.ds(mate[k] * per, per)], xs.at[k], a_send.at[k], a_recv.at[k], mate[k], z)

    def strip_copy(h, s):
        a, b = strips[s]
        k = 2 * far + h
        return remote(
            pix.at[pl.ds(mate[k] * per, per), pl.ds(a, b - a)], xs.at[k, :, pl.ds(a, b - a)],
            d_send.at[h, s], d_recv.at[h, s], mate[k], z,
        )

    early = [1] + list(range(2, 2 * far, 2)) + list(range(3, 2 * far, 2))
    for k in early:
        whole(k).start()

    def split(k, a, b):
        at = k % 2 * block
        for p in range(per):
            x = xs[k, p, a:b]
            h = x.astype(jnp.bfloat16)
            hi[k // 2, at + a:at + b, p * depth:(p + 1) * depth] = h
            lo[k // 2, at + a:at + b, p * depth:(p + 1) * depth] = (x - h.astype(jnp.float32)).astype(jnp.bfloat16)

    def joined(left, right):
        other = jnp.concatenate([right[:, block:], right[:, :block]], axis=1)
        return left + other

    def pair_copy(n):
        return remote(part.at[n, 1], pair_in.at[n], p_send.at[n], p_recv.at[n], mate[1], z)

    def z_copy(n):
        t, slot = EARLY[PAIRS[n]]
        k = differ(z, near[t], zbits)
        return near[t], remote(summed.at[n], z_in.at[k, slot], z_send.at[n], z_recv.at[k, slot], r, near[t])

    def product(n):
        i, j = PAIRS[n]
        value = dot_t(hi[i], hi[j]) + dot_t(hi[i], lo[j]) + dot_t(lo[i], hi[j])
        part[n, 0] = value[:block]
        part[n, 1] = value[block:]
        pair_copy(n).start()

    def finish(n):
        pair_copy(n).wait_recv()
        summed[n] = joined(part[n, 0], pair_in[n])
        plane, copy = z_copy(n)

        @pl.when(plane != z)
        def _():
            copy.start()

    def row_of(chip_at, half):
        return 2 * chip_at + (core if half == 0 else 1 - core)

    def direct_copy(n):
        i, j = PAIRS[n]
        slot = EARLY[PAIRS[n]][1]
        to = 1 if (i, j) == (2, 2) else 0
        return remote(esum.at[slot], ed_in.at[to], e_send.at[slot], e_recv.at[to], row_of(near[i], 0), near[j])

    def mirror_copy(n, half):
        i, j = PAIRS[n]
        slot = EARLY[PAIRS[n]][1]
        return remote(
            esum.at[slot, :, pl.ds(half * block, block)], em_in.at[half],
            em_send.at[slot, half], em_recv.at[half], row_of(near[j], half), near[i],
        )

    def each_early(action):
        for t in range(chips):
            @pl.when(mine == t)
            def _():
                for n, pair in enumerate(PAIRS):
                    if EARLY[pair][0] == t:
                        action(n)

    def gather_early(n):
        slot = EARLY[PAIRS[n]][1]
        total = summed[n]
        for k in range(1, cols):
            remote(summed.at[n], z_in.at[k, slot], z_send.at[n], z_recv.at[k, slot], r, zs[k]).wait_recv()
            total = total + z_in[k, slot]
        esum[slot] = total
        i, j = PAIRS[n]
        if i > 0:
            direct_copy(n).start()
        if i != j:
            for half in range(2):
                mirror_copy(n, half).start()

    def drain_early(n):
        i, j = PAIRS[n]
        if i > 0:
            direct_copy(n).wait_send()
        if i != j:
            for half in range(2):
                mirror_copy(n, half).wait_send()

    def strip_product(s):
        a, b = strips[s]
        m = b - a
        h = jnp.concatenate([hi[far, a:b], hi[far, block + a:block + b]], axis=0)
        both = jnp.concatenate([h, lo[far, a:b], lo[far, block + a:block + b]], axis=0)
        for j in range(chips):
            value = dot_t(both, hi[j])
            value = value[:2 * m] + value[2 * m:] + dot_t(h, lo[j])
            lpart[j, 0, a:b] = value[:m]
            lpart[j, 1, a:b] = value[m:]

    def late_pair(s):
        a, b = strips[s]
        rng = pl.ds(a, b - a)
        return remote(lpart.at[:, 1, rng], lpair.at[:, rng], lp_send.at[s], lp_recv.at[s], mate[1], z)

    def late_z(s, k):
        a, b = strips[s]
        rng = pl.ds(a, b - a)
        return remote(
            lsum.at[differ(mine, k, zbits), rng], lz_in.at[k, rng], lz_send.at[k, s], lz_recv.at[k, s], r, zs[k]
        )

    def late_direct(s):
        a, b = strips[s]
        rng = pl.ds(a, b - a)
        return remote(lout.at[rng], ld_in.at[rng], ld_send.at[s], ld_recv.at[s], row_of(near[far], 0), z)

    def late_mirror(s, half):
        a, b = strips[s]
        rng = pl.ds(a, b - a)
        return remote(
            lout.at[rng, pl.ds(half * block, block)], lm_in.at[half, rng],
            lm_send.at[half, s], lm_recv.at[half, s], row_of(z, half), near[far],
        )

    def late_finish(s):
        a, b = strips[s]
        late_pair(s).wait_recv()
        for j in range(chips):
            lsum[j, a:b] = joined(lpart[j, 0, a:b], lpair[j, a:b])
        for k in range(cols - 1, 0, -1):
            late_z(s, k).start()

    def late_gather(s):
        a, b = strips[s]
        total = lsum[mine, a:b]
        for k in range(1, cols):
            late_z(s, k).wait_recv()
            total = total + lz_in[k, a:b]
        lout[a:b] = total
        for half in range(2):
            late_mirror(s, half).start()
        late_direct(s).start()

    own.wait()
    split(0, 0, block)
    whole(1).wait_recv()
    split(1, 0, block)
    product(0)
    finish(0)
    for k in early[1:]:
        whole(k).wait_send()
    for s in range(2):
        for h in range(2):
            strip_copy(h, s).start()
    for g in range(1, far):
        for k in (2 * g, 2 * g + 1):
            whole(k).wait_recv()
            split(k, 0, block)
        fresh = [n for n, pair in enumerate(PAIRS) if pair[0] == g]
        for n in fresh:
            product(n)
        for n in fresh:
            finish(n)

    for s, (a, b) in enumerate(strips):
        for h in range(2):
            strip_copy(h, s).wait_recv()
        if s + 2 < len(strips):
            for h in range(2):
                strip_copy(h, s).wait_send()
            for h in range(2):
                strip_copy(h, s + 2).start()
        for h in range(2):
            split(2 * far + h, a, b)
        strip_product(s)
        late_pair(s).start()
        if s > 0:
            late_gather(s - 1)
        late_finish(s)
        if s == len(strips) - 3:
            each_early(gather_early)
    late_gather(len(strips) - 1)

    remote(esum.at[0], ed_in.at[0], e_send.at[0], e_recv.at[0], mate[1], z).wait_recv()

    @pl.when(mine == 0)
    def _():
        remote(esum.at[0], ed_in.at[1], e_send.at[0], e_recv.at[1], mate[1], z).wait_recv()
        work[...] = esum[0] + ed_in[0] + ed_in[1]

    @pl.when(mine != 0)
    def _():
        for half in range(2):
            remote(
                esum.at[0, :, pl.ds(half * block, block)], em_in.at[half], em_send.at[0, half], em_recv.at[half], mate[1], z
            ).wait_recv()
            at = slice(half * block, (half + 1) * block)
            work[:, at] = ed_in[0, :, at] + em_in[half].T

    for s in range(len(strips)):
        late_direct(s).wait_recv()
        for half in range(2):
            late_mirror(s, half).wait_recv()
    row = lax.broadcasted_iota(jnp.int32, (block, block), 0)
    column = lax.broadcasted_iota(jnp.int32, (block, block), 1)
    start = jnp.zeros((block, block), jnp.int32)
    for a, b in strips:
        start = jnp.where(column >= a, a, start)
    keep = jnp.logical_or(row < start, mine != 0)
    for half in range(2):
        at = slice(half * block, (half + 1) * block)
        mirrored = jnp.where(keep, lm_in[half].T, 0.0)
        total = (work[:, at] + ld_in[:, at] + mirrored) * scale
        to = core * block if half == 0 else (1 - core) * block
        gram[:, pl.ds(pl.multiple_of(to, block), block)] = total

    value = lax.dot_general(
        fac[...], gram[...], (((0,), (0,)), ((), ())),
        precision=lax.Precision.HIGHEST, preferred_element_type=jnp.float32,
    )
    share = value.shape[0] // rows
    for k in range(rows):
        term[k] = value[k * share:(k + 1) * share]

    def term_copy(k):
        return remote(term.at[mate[k]], term_in.at[k], t_send.at[k], t_recv.at[k], mate[k], z)

    for k in range(rows - 1, 0, -1):
        term_copy(k).start()
    total = term[r]
    for k in range(1, rows):
        term_copy(k).wait_recv()
        total = total + term_in[k]
    proj[...] = total

    whole(1).wait_send()
    for k in range(1, rows):
        term_copy(k).wait_send()
    for n in range(len(PAIRS)):
        pair_copy(n).wait_send()
        plane, copy = z_copy(n)

        @pl.when(plane != z)
        def _():
            copy.wait_send()
    each_early(drain_early)
    for s in range(len(strips)):
        if s + 2 >= len(strips):
            for h in range(2):
                strip_copy(h, s).wait_send()
        late_pair(s).wait_send()
        for k in range(1, cols):
            late_z(s, k).wait_send()
        late_direct(s).wait_send()
        for half in range(2):
            late_mirror(s, half).wait_send()


def hand_on(gram, proj, gram_out, proj_out):
    gram_out[...] = gram[...]
    proj_out[...] = proj[...]


def fused(pixels, factor):
    rows, cols = lax.axis_size("row"), lax.axis_size("col")
    views, colours, block, depth = pixels.shape
    count = views * colours
    per = count // rows
    chips = rows // 2
    rank = factor.shape[1]
    scale = 1.0 / (count * depth * cols)
    unit = block // 8
    cuts = (0, 3 * unit, 5 * unit, 7 * unit, block)
    n = len(cuts) - 1
    pairs = len(PAIRS)
    vmem, dma = pltpu.VMEM, pltpu.SemaphoreType.DMA
    f32 = jnp.float32
    in_vmem = pl.BlockSpec(memory_space=pltpu.VMEM)
    shapes = (
        jax.ShapeDtypeStruct((block, 2 * block), f32),
        jax.ShapeDtypeStruct((rank // rows, 2 * block), f32),
    )
    gram, proj = pl.pallas_call(
        functools.partial(kernel, rows, cols, scale, cuts),
        out_shape=shapes,
        in_specs=[pl.BlockSpec(memory_space=pl.ANY), in_vmem],
        out_specs=(in_vmem, in_vmem),
        scratch_shapes=[
            vmem((rows, per, block, depth), f32),
            vmem((chips, 2 * block, per * depth), jnp.bfloat16),
            vmem((chips, 2 * block, per * depth), jnp.bfloat16),
            vmem((pairs, 2, block, 2 * block), f32),
            vmem((pairs, block, 2 * block), f32),
            vmem((pairs, block, 2 * block), f32),
            vmem((cols, SLOTS, block, 2 * block), f32),
            vmem((SLOTS, block, 2 * block), f32),
            vmem((2, block, 2 * block), f32),
            vmem((2, block, block), f32),
            vmem((chips, 2, block, 2 * block), f32),
            vmem((chips, block, 2 * block), f32),
            vmem((chips, block, 2 * block), f32),
            vmem((cols, block, 2 * block), f32),
            vmem((block, 2 * block), f32),
            vmem((block, 2 * block), f32),
            vmem((2, block, block), f32),
            vmem((block, 2 * block), f32),
            vmem((rows, rank // rows, 2 * block), f32),
            vmem((rows, rank // rows, 2 * block), f32),
            dma,
            dma((rows,)), dma((rows,)),
            dma((2, n)), dma((2, n)),
            dma((pairs,)), dma((pairs,)),
            dma((pairs,)), dma((cols, SLOTS)),
            dma((SLOTS,)), dma((2,)),
            dma((SLOTS, 2)), dma((2,)),
            dma((n,)), dma((n,)),
            dma((cols, n)), dma((cols, n)),
            dma((n,)), dma((n,)),
            dma((2, n)), dma((2, n)),
            dma((rows,)), dma((rows,)),
        ],
        compiler_params=pltpu.CompilerParams(
            collective_id=0, has_side_effects=True, vmem_limit_bytes=56 * 1024 * 1024
        ),
    )(pixels.reshape(count, block, depth), factor)
    gram, proj = pl.pallas_call(hand_on, out_shape=shapes, in_specs=[in_vmem] * 2, out_specs=(in_vmem, in_vmem))(gram, proj)
    return gram, proj.T


def pair_rows(own, others):
    return jnp.einsum(
        "vciw,vcjw->ij", own, others, precision=lax.Precision.HIGHEST, preferred_element_type=jnp.float32
    )


def general(pixels, factor):
    col_count = lax.axis_size("col")
    row_count = lax.axis_size("row")
    weight_scale = 1.0 / (pixels.shape[0] * pixels.shape[1] * pixels.shape[3] * col_count)
    row_block = pixels.shape[2]
    slices = lax.all_to_all(pixels, "row", split_axis=3, concat_axis=2, tiled=True)
    partial_value = pair_rows(slices, slices) * weight_scale
    width = partial_value.shape[0] // col_count
    arranged = partial_value.reshape(row_count, row_block, col_count, width)
    arranged = jnp.transpose(arranged, (0, 2, 1, 3)).reshape(row_count * col_count * row_block, width)
    block = lax.psum_scatter(arranged, ("row", "col"), scatter_dimension=0, tiled=True)
    term = lax.dot_general(
        block, factor, (((0,), (0,)), ((), ())),
        precision=lax.Precision.HIGHEST, preferred_element_type=jnp.float32,
    )
    summed_term = lax.psum(term, "row")
    share = summed_term.shape[1] // row_count
    projected = lax.dynamic_slice_in_dim(summed_term, lax.axis_index("row") * share, share, 1)
    return (block, projected)


def shards(pixels, factor):
    rows, cols = lax.axis_size("row"), lax.axis_size("col")
    views, colours, block, depth = pixels.shape
    fits = (
        rows == 2 * cols
        and cols == len({t for t, _ in EARLY.values()})
        and (views * colours) % rows == 0
        and block % 128 == 0
        and depth % 128 == 0
        and factor.shape[1] % (8 * rows) == 0
        and 8 * rows * block * (views * colours // rows) * depth <= 16 * 1024 * 1024
    )
    return (fused if fits else general)(pixels, factor)


def solution(mesh):
    in_specs = (P(None, None, "row", "col"), P("row", None))
    out_specs = (P("row", "col"), P("col", "row"))
    return jax.shard_map(shards, mesh=mesh, in_specs=in_specs, out_specs=out_specs, check_vma=False)
```

```python
import functools

import jax
import jax.numpy as jnp
from jax import lax
from jax.experimental import pallas as pl
from jax.experimental.pallas import tpu as pltpu
from jax.sharding import PartitionSpec as P

MESH = pl.DeviceIdType.MESH

EARLY = {(0, 0): (0, 0), (1, 0): (0, 1), (1, 1): (1, 0), (2, 0): (1, 1), (2, 1): (3, 0), (2, 2): (2, 0)}
PAIRS = list(EARLY)
SLOTS = 2


def flip(value, mask, bits):
    out = 0
    for b in range(bits):
        bit = (value // (1 << b)) % 2
        out = out + (1 << b) * ((1 - bit) if (mask >> b) & 1 else bit)
    return out


def differ(left, right, bits):
    out = 0
    for b in range(bits):
        out = out + (1 << b) * (((left // (1 << b)) + (right // (1 << b))) % 2)
    return out


def dot_t(a, b):
    return lax.dot_general(a, b, (((1,), (1,)), ((), ())), preferred_element_type=jnp.float32)


def kernel(
    rows, cols, scale, cuts,
    pix, fac, gram, proj,
    xs, hi, lo, part, pair_in, summed, z_in, esum, ed_in, em_in,
    lpart, lpair, lsum, lz_in, lout, ld_in, lm_in, work, term, term_in,
    own_sem, a_send, a_recv, d_send, d_recv, p_send, p_recv, z_send, z_recv, e_send, e_recv, em_send, em_recv,
    lp_send, lp_recv, lz_send, lz_recv, ld_send, ld_recv, lm_send, lm_recv, t_send, t_recv,
):
    r = lax.axis_index("row")
    z = lax.axis_index("col")
    core = r % 2
    chip = r // 2
    rbits = rows.bit_length() - 1
    zbits = cols.bit_length() - 1
    chips = rows // 2
    far = chips - 1
    mine = differ(chip, z, zbits)
    per = pix.shape[0] // rows
    block = pix.shape[1]
    depth = pix.shape[2]
    mate = [flip(r, k, rbits) for k in range(rows)]
    zs = [flip(z, k, zbits) for k in range(cols)]
    near = [flip(chip, i, zbits) for i in range(chips)]
    strips = list(zip(cuts[:-1], cuts[1:]))

    def remote(src, dst, send, recv, row, plane):
        return pltpu.make_async_remote_copy(
            src_ref=src, dst_ref=dst, send_sem=send, recv_sem=recv, device_id=(row, plane), device_id_type=MESH
        )

    barrier = pltpu.get_barrier_semaphore()
    for k in range(rows):
        for kz in range(cols):
            if (k == 0) != (kz == 0):
                pl.semaphore_signal(barrier, inc=1, device_id=(mate[k], zs[kz]), device_id_type=MESH)
    own = pltpu.make_async_copy(pix.at[pl.ds(r * per, per)], xs.at[0], own_sem)
    own.start()
    hi[far] = jnp.zeros(hi.shape[1:], hi.dtype)
    lo[far] = jnp.zeros(lo.shape[1:], lo.dtype)
    pl.semaphore_wait(barrier, rows + cols - 2)

    def whole(k):
        return remote(pix.at[pl.ds(mate[k] * per, per)], xs.at[k], a_send.at[k], a_recv.at[k], mate[k], z)

    def strip_copy(h, s):
        a, b = strips[s]
        k = 2 * far + h
        return remote(
            pix.at[pl.ds(mate[k] * per, per), pl.ds(a, b - a)], xs.at[k, :, pl.ds(a, b - a)],
            d_send.at[h, s], d_recv.at[h, s], mate[k], z,
        )

    early = [1] + list(range(2, 2 * far, 2)) + list(range(3, 2 * far, 2))
    for k in early:
        whole(k).start()

    def split(k, a, b):
        at = k % 2 * block
        for p in range(per):
            x = xs[k, p, a:b]
            h = x.astype(jnp.bfloat16)
            hi[k // 2, at + a:at + b, p * depth:(p + 1) * depth] = h
            lo[k // 2, at + a:at + b, p * depth:(p + 1) * depth] = (x - h.astype(jnp.float32)).astype(jnp.bfloat16)

    def joined(left, right):
        other = jnp.concatenate([right[:, block:], right[:, :block]], axis=1)
        return left + other

    def pair_copy(n):
        return remote(part.at[n, 1], pair_in.at[n], p_send.at[n], p_recv.at[n], mate[1], z)

    def z_copy(n):
        t, slot = EARLY[PAIRS[n]]
        k = differ(z, near[t], zbits)
        return near[t], remote(summed.at[n], z_in.at[k, slot], z_send.at[n], z_recv.at[k, slot], r, near[t])

    def product(n):
        i, j = PAIRS[n]
        value = dot_t(hi[i], hi[j]) + dot_t(hi[i], lo[j]) + dot_t(lo[i], hi[j])
        part[n, 0] = value[:block]
        part[n, 1] = value[block:]
        pair_copy(n).start()

    def finish(n):
        pair_copy(n).wait_recv()
        summed[n] = joined(part[n, 0], pair_in[n])
        plane, copy = z_copy(n)

        @pl.when(plane != z)
        def _():
            copy.start()

    def row_of(chip_at, half):
        return 2 * chip_at + (core if half == 0 else 1 - core)

    def direct_copy(n):
        i, j = PAIRS[n]
        slot = EARLY[PAIRS[n]][1]
        to = 1 if (i, j) == (2, 2) else 0
        return remote(esum.at[slot], ed_in.at[to], e_send.at[slot], e_recv.at[to], row_of(near[i], 0), near[j])

    def mirror_copy(n, half):
        i, j = PAIRS[n]
        slot = EARLY[PAIRS[n]][1]
        return remote(
            esum.at[slot, :, pl.ds(half * block, block)], em_in.at[half],
            em_send.at[slot, half], em_recv.at[half], row_of(near[j], half), near[i],
        )

    def each_early(action):
        for t in range(chips):
            @pl.when(mine == t)
            def _():
                for n, pair in enumerate(PAIRS):
                    if EARLY[pair][0] == t:
                        action(n)

    def gather_early(n):
        slot = EARLY[PAIRS[n]][1]
        total = summed[n]
        for k in range(1, cols):
            remote(summed.at[n], z_in.at[k, slot], z_send.at[n], z_recv.at[k, slot], r, zs[k]).wait_recv()
            total = total + z_in[k, slot]
        esum[slot] = total
        i, j = PAIRS[n]
        if i > 0:
            direct_copy(n).start()
        if i != j:
            for half in range(2):
                mirror_copy(n, half).start()

    def drain_early(n):
        i, j = PAIRS[n]
        if i > 0:
            direct_copy(n).wait_send()
        if i != j:
            for half in range(2):
                mirror_copy(n, half).wait_send()

    def strip_product(s):
        a, b = strips[s]
        m = b - a
        h = jnp.concatenate([hi[far, a:b], hi[far, block + a:block + b]], axis=0)
        both = jnp.concatenate([h, lo[far, a:b], lo[far, block + a:block + b]], axis=0)
        for j in range(chips):
            value = dot_t(both, hi[j])
            value = value[:2 * m] + value[2 * m:] + dot_t(h, lo[j])
            lpart[j, 0, a:b] = value[:m]
            lpart[j, 1, a:b] = value[m:]

    def late_pair(s):
        a, b = strips[s]
        rng = pl.ds(a, b - a)
        return remote(lpart.at[:, 1, rng], lpair.at[:, rng], lp_send.at[s], lp_recv.at[s], mate[1], z)

    def late_z(s, k):
        a, b = strips[s]
        rng = pl.ds(a, b - a)
        return remote(
            lsum.at[differ(mine, k, zbits), rng], lz_in.at[k, rng], lz_send.at[k, s], lz_recv.at[k, s], r, zs[k]
        )

    def late_direct(s):
        a, b = strips[s]
        rng = pl.ds(a, b - a)
        return remote(lout.at[rng], ld_in.at[rng], ld_send.at[s], ld_recv.at[s], row_of(near[far], 0), z)

    def late_mirror(s, half):
        a, b = strips[s]
        rng = pl.ds(a, b - a)
        return remote(
            lout.at[rng, pl.ds(half * block, block)], lm_in.at[half, rng],
            lm_send.at[half, s], lm_recv.at[half, s], row_of(z, half), near[far],
        )

    def late_finish(s):
        a, b = strips[s]
        late_pair(s).wait_recv()
        for j in range(chips):
            lsum[j, a:b] = joined(lpart[j, 0, a:b], lpair[j, a:b])
        for k in range(cols - 1, 0, -1):
            late_z(s, k).start()

    def late_gather(s):
        a, b = strips[s]
        total = lsum[mine, a:b]
        for k in range(1, cols):
            late_z(s, k).wait_recv()
            total = total + lz_in[k, a:b]
        lout[a:b] = total
        for half in range(2):
            late_mirror(s, half).start()
        late_direct(s).start()

    own.wait()
    split(0, 0, block)
    whole(1).wait_recv()
    split(1, 0, block)
    product(0)
    finish(0)
    for k in early[1:]:
        whole(k).wait_send()
    for s in range(2):
        for h in range(2):
            strip_copy(h, s).start()
    for g in range(1, far):
        for k in (2 * g, 2 * g + 1):
            whole(k).wait_recv()
            split(k, 0, block)
        fresh = [n for n, pair in enumerate(PAIRS) if pair[0] == g]
        for n in fresh:
            product(n)
        for n in fresh:
            finish(n)

    for s, (a, b) in enumerate(strips):
        for h in range(2):
            strip_copy(h, s).wait_recv()
        if s + 2 < len(strips):
            for h in range(2):
                strip_copy(h, s).wait_send()
            for h in range(2):
                strip_copy(h, s + 2).start()
        for h in range(2):
            split(2 * far + h, a, b)
        strip_product(s)
        late_pair(s).start()
        late_finish(s)
        if s > 0:
            late_gather(s - 1)
        if s == len(strips) - 3:
            each_early(gather_early)
    late_gather(len(strips) - 1)

    remote(esum.at[0], ed_in.at[0], e_send.at[0], e_recv.at[0], mate[1], z).wait_recv()

    @pl.when(mine == 0)
    def _():
        remote(esum.at[0], ed_in.at[1], e_send.at[0], e_recv.at[1], mate[1], z).wait_recv()
        work[...] = esum[0] + ed_in[0] + ed_in[1]

    @pl.when(mine != 0)
    def _():
        for half in range(2):
            remote(
                esum.at[0, :, pl.ds(half * block, block)], em_in.at[half], em_send.at[0, half], em_recv.at[half], mate[1], z
            ).wait_recv()
            at = slice(half * block, (half + 1) * block)
            work[:, at] = ed_in[0, :, at] + em_in[half].T

    for s in range(len(strips)):
        late_direct(s).wait_recv()
        for half in range(2):
            late_mirror(s, half).wait_recv()
    row = lax.broadcasted_iota(jnp.int32, (block, block), 0)
    column = lax.broadcasted_iota(jnp.int32, (block, block), 1)
    start = jnp.zeros((block, block), jnp.int32)
    for a, b in strips:
        start = jnp.where(column >= a, a, start)
    keep = jnp.logical_or(row < start, mine != 0)
    for half in range(2):
        at = slice(half * block, (half + 1) * block)
        mirrored = jnp.where(keep, lm_in[half].T, 0.0)
        total = (work[:, at] + ld_in[:, at] + mirrored) * scale
        to = core * block if half == 0 else (1 - core) * block
        gram[:, pl.ds(pl.multiple_of(to, block), block)] = total

    value = lax.dot_general(
        fac[...], gram[...], (((0,), (0,)), ((), ())),
        precision=lax.Precision.HIGHEST, preferred_element_type=jnp.float32,
    )
    share = value.shape[0] // rows
    for k in range(rows):
        term[k] = value[k * share:(k + 1) * share]

    def term_copy(k):
        return remote(term.at[mate[k]], term_in.at[k], t_send.at[k], t_recv.at[k], mate[k], z)

    for k in range(rows - 1, 0, -1):
        term_copy(k).start()
    total = term[r]
    for k in range(1, rows):
        term_copy(k).wait_recv()
        total = total + term_in[k]
    proj[...] = total

    whole(1).wait_send()
    for k in range(1, rows):
        term_copy(k).wait_send()
    for n in range(len(PAIRS)):
        pair_copy(n).wait_send()
        plane, copy = z_copy(n)

        @pl.when(plane != z)
        def _():
            copy.wait_send()
    each_early(drain_early)
    for s in range(len(strips)):
        if s + 2 >= len(strips):
            for h in range(2):
                strip_copy(h, s).wait_send()
        late_pair(s).wait_send()
        for k in range(1, cols):
            late_z(s, k).wait_send()
        late_direct(s).wait_send()
        for half in range(2):
            late_mirror(s, half).wait_send()


def hand_on(gram, proj, gram_out, proj_out):
    gram_out[...] = gram[...]
    proj_out[...] = proj[...]


def fused(pixels, factor):
    rows, cols = lax.axis_size("row"), lax.axis_size("col")
    views, colours, block, depth = pixels.shape
    count = views * colours
    per = count // rows
    chips = rows // 2
    rank = factor.shape[1]
    scale = 1.0 / (count * depth * cols)
    unit = block // 8
    cuts = (0, 4 * unit, 6 * unit, 7 * unit, block)
    n = len(cuts) - 1
    pairs = len(PAIRS)
    vmem, dma = pltpu.VMEM, pltpu.SemaphoreType.DMA
    f32 = jnp.float32
    in_vmem = pl.BlockSpec(memory_space=pltpu.VMEM)
    shapes = (
        jax.ShapeDtypeStruct((block, 2 * block), f32),
        jax.ShapeDtypeStruct((rank // rows, 2 * block), f32),
    )
    gram, proj = pl.pallas_call(
        functools.partial(kernel, rows, cols, scale, cuts),
        out_shape=shapes,
        in_specs=[pl.BlockSpec(memory_space=pl.ANY), in_vmem],
        out_specs=(in_vmem, in_vmem),
        scratch_shapes=[
            vmem((rows, per, block, depth), f32),
            vmem((chips, 2 * block, per * depth), jnp.bfloat16),
            vmem((chips, 2 * block, per * depth), jnp.bfloat16),
            vmem((pairs, 2, block, 2 * block), f32),
            vmem((pairs, block, 2 * block), f32),
            vmem((pairs, block, 2 * block), f32),
            vmem((cols, SLOTS, block, 2 * block), f32),
            vmem((SLOTS, block, 2 * block), f32),
            vmem((2, block, 2 * block), f32),
            vmem((2, block, block), f32),
            vmem((chips, 2, block, 2 * block), f32),
            vmem((chips, block, 2 * block), f32),
            vmem((chips, block, 2 * block), f32),
            vmem((cols, block, 2 * block), f32),
            vmem((block, 2 * block), f32),
            vmem((block, 2 * block), f32),
            vmem((2, block, block), f32),
            vmem((block, 2 * block), f32),
            vmem((rows, rank // rows, 2 * block), f32),
            vmem((rows, rank // rows, 2 * block), f32),
            dma,
            dma((rows,)), dma((rows,)),
            dma((2, n)), dma((2, n)),
            dma((pairs,)), dma((pairs,)),
            dma((pairs,)), dma((cols, SLOTS)),
            dma((SLOTS,)), dma((2,)),
            dma((SLOTS, 2)), dma((2,)),
            dma((n,)), dma((n,)),
            dma((cols, n)), dma((cols, n)),
            dma((n,)), dma((n,)),
            dma((2, n)), dma((2, n)),
            dma((rows,)), dma((rows,)),
        ],
        compiler_params=pltpu.CompilerParams(
            collective_id=0, has_side_effects=True, vmem_limit_bytes=56 * 1024 * 1024
        ),
    )(pixels.reshape(count, block, depth), factor)
    gram, proj = pl.pallas_call(hand_on, out_shape=shapes, in_specs=[in_vmem] * 2, out_specs=(in_vmem, in_vmem))(gram, proj)
    return gram, proj.T


def pair_rows(own, others):
    return jnp.einsum(
        "vciw,vcjw->ij", own, others, precision=lax.Precision.HIGHEST, preferred_element_type=jnp.float32
    )


def general(pixels, factor):
    col_count = lax.axis_size("col")
    row_count = lax.axis_size("row")
    weight_scale = 1.0 / (pixels.shape[0] * pixels.shape[1] * pixels.shape[3] * col_count)
    row_block = pixels.shape[2]
    slices = lax.all_to_all(pixels, "row", split_axis=3, concat_axis=2, tiled=True)
    partial_value = pair_rows(slices, slices) * weight_scale
    width = partial_value.shape[0] // col_count
    arranged = partial_value.reshape(row_count, row_block, col_count, width)
    arranged = jnp.transpose(arranged, (0, 2, 1, 3)).reshape(row_count * col_count * row_block, width)
    block = lax.psum_scatter(arranged, ("row", "col"), scatter_dimension=0, tiled=True)
    term = lax.dot_general(
        block, factor, (((0,), (0,)), ((), ())),
        precision=lax.Precision.HIGHEST, preferred_element_type=jnp.float32,
    )
    summed_term = lax.psum(term, "row")
    share = summed_term.shape[1] // row_count
    projected = lax.dynamic_slice_in_dim(summed_term, lax.axis_index("row") * share, share, 1)
    return (block, projected)


def shards(pixels, factor):
    rows, cols = lax.axis_size("row"), lax.axis_size("col")
    views, colours, block, depth = pixels.shape
    fits = (
        rows == 2 * cols
        and cols == len({t for t, _ in EARLY.values()})
        and (views * colours) % rows == 0
        and block % 128 == 0
        and depth % 128 == 0
        and factor.shape[1] % (8 * rows) == 0
        and 8 * rows * block * (views * colours // rows) * depth <= 16 * 1024 * 1024
    )
    return (fused if fits else general)(pixels, factor)


def solution(mesh):
    in_specs = (P(None, None, "row", "col"), P("row", None))
    out_specs = (P("row", "col"), P("col", "row"))
    return jax.shard_map(shards, mesh=mesh, in_specs=in_specs, out_specs=out_specs, check_vma=False)
```

```python
import functools

import jax
import jax.numpy as jnp
from jax import lax
from jax.experimental import pallas as pl
from jax.experimental.pallas import tpu as pltpu
from jax.sharding import PartitionSpec as P

MESH = pl.DeviceIdType.MESH

EARLY = {(0, 0): (0, 0), (1, 0): (0, 1), (1, 1): (1, 0), (2, 0): (1, 1), (2, 1): (3, 0), (2, 2): (2, 0)}
PAIRS = list(EARLY)
SLOTS = 2


def flip(value, mask, bits):
    out = 0
    for b in range(bits):
        bit = (value // (1 << b)) % 2
        out = out + (1 << b) * ((1 - bit) if (mask >> b) & 1 else bit)
    return out


def differ(left, right, bits):
    out = 0
    for b in range(bits):
        out = out + (1 << b) * (((left // (1 << b)) + (right // (1 << b))) % 2)
    return out


def dot_t(a, b):
    return lax.dot_general(a, b, (((1,), (1,)), ((), ())), preferred_element_type=jnp.float32)


def kernel(
    rows, cols, scale, cuts,
    pix, fac, gram, proj,
    xs, hi, lo, part, pair_in, summed, z_in, esum, ed_in, em_in,
    lpart, lpair, lsum, lz_in, lout, ld_in, lm_in, work, fown, fout, fmate, gmate, term, term_in,
    own_sem, a_send, a_recv, d_send, d_recv, p_send, p_recv, z_send, z_recv, e_send, e_recv, em_send, em_recv,
    lp_send, lp_recv, lz_send, lz_recv, ld_send, ld_recv, lm_send, lm_recv, f_sem, g_sem, t_send, t_recv,
):
    r = lax.axis_index("row")
    z = lax.axis_index("col")
    core = r % 2
    chip = r // 2
    rbits = rows.bit_length() - 1
    zbits = cols.bit_length() - 1
    chips = rows // 2
    far = chips - 1
    mine = differ(chip, z, zbits)
    per = pix.shape[0] // rows
    block = pix.shape[1]
    depth = pix.shape[2]
    mate = [flip(r, k, rbits) for k in range(rows)]
    zs = [flip(z, k, zbits) for k in range(cols)]
    near = [flip(chip, i, zbits) for i in range(chips)]
    strips = list(zip(cuts[:-1], cuts[1:]))

    def remote(src, dst, send, recv, row, plane):
        return pltpu.make_async_remote_copy(
            src_ref=src, dst_ref=dst, send_sem=send, recv_sem=recv, device_id=(row, plane), device_id_type=MESH
        )

    barrier = pltpu.get_barrier_semaphore()
    for k in range(rows):
        for kz in range(cols):
            if (k == 0) != (kz == 0):
                pl.semaphore_signal(barrier, inc=1, device_id=(mate[k], zs[kz]), device_id_type=MESH)
    own = pltpu.make_async_copy(pix.at[pl.ds(r * per, per)], xs.at[0], own_sem)
    own.start()
    hi[far] = jnp.zeros(hi.shape[1:], hi.dtype)
    lo[far] = jnp.zeros(lo.shape[1:], lo.dtype)
    pl.semaphore_wait(barrier, rows + cols - 2)

    def whole(k):
        return remote(pix.at[pl.ds(mate[k] * per, per)], xs.at[k], a_send.at[k], a_recv.at[k], mate[k], z)

    def strip_copy(h, s):
        a, b = strips[s]
        k = 2 * far + h
        return remote(
            pix.at[pl.ds(mate[k] * per, per), pl.ds(a, b - a)], xs.at[k, :, pl.ds(a, b - a)],
            d_send.at[h, s], d_recv.at[h, s], mate[k], z,
        )

    share = fac.shape[1] // rows
    for i in range(chips):
        even = fac[:, 2 * i * share:(2 * i + 1) * share]
        odd = fac[:, (2 * i + 1) * share:(2 * i + 2) * share]
        fown[:, i * share:(i + 1) * share] = jnp.where(core == 0, even, odd)
        fout[:, i * share:(i + 1) * share] = jnp.where(core == 0, odd, even)

    early = [1] + list(range(2, 2 * far, 2)) + list(range(3, 2 * far, 2))
    for k in early:
        whole(k).start()
    factor_copy = remote(fout, fmate, f_sem.at[0], f_sem.at[1], mate[1], z)
    factor_copy.start()

    def split(k, a, b):
        at = k % 2 * block
        for p in range(per):
            x = xs[k, p, a:b]
            h = x.astype(jnp.bfloat16)
            hi[k // 2, at + a:at + b, p * depth:(p + 1) * depth] = h
            lo[k // 2, at + a:at + b, p * depth:(p + 1) * depth] = (x - h.astype(jnp.float32)).astype(jnp.bfloat16)

    def joined(left, right):
        other = jnp.concatenate([right[:, block:], right[:, :block]], axis=1)
        return left + other

    def pair_copy(n):
        return remote(part.at[n, 1], pair_in.at[n], p_send.at[n], p_recv.at[n], mate[1], z)

    def z_copy(n):
        t, slot = EARLY[PAIRS[n]]
        k = differ(z, near[t], zbits)
        return near[t], remote(summed.at[n], z_in.at[k, slot], z_send.at[n], z_recv.at[k, slot], r, near[t])

    def product(n):
        i, j = PAIRS[n]
        value = dot_t(hi[i], hi[j]) + dot_t(hi[i], lo[j]) + dot_t(lo[i], hi[j])
        part[n, 0] = value[:block]
        part[n, 1] = value[block:]
        pair_copy(n).start()

    def finish(n):
        pair_copy(n).wait_recv()
        summed[n] = joined(part[n, 0], pair_in[n])
        plane, copy = z_copy(n)

        @pl.when(plane != z)
        def _():
            copy.start()

    def row_of(chip_at, half):
        return 2 * chip_at + (core if half == 0 else 1 - core)

    def direct_copy(n):
        i, j = PAIRS[n]
        slot = EARLY[PAIRS[n]][1]
        to = 1 if (i, j) == (2, 2) else 0
        return remote(esum.at[slot], ed_in.at[to], e_send.at[slot], e_recv.at[to], row_of(near[i], 0), near[j])

    def mirror_copy(n, half):
        i, j = PAIRS[n]
        slot = EARLY[PAIRS[n]][1]
        return remote(
            esum.at[slot, :, pl.ds(half * block, block)], em_in.at[half],
            em_send.at[slot, half], em_recv.at[half], row_of(near[j], half), near[i],
        )

    def each_early(action):
        for t in range(chips):
            @pl.when(mine == t)
            def _():
                for n, pair in enumerate(PAIRS):
                    if EARLY[pair][0] == t:
                        action(n)

    def gather_early(n):
        slot = EARLY[PAIRS[n]][1]
        total = summed[n]
        for k in range(1, cols):
            remote(summed.at[n], z_in.at[k, slot], z_send.at[n], z_recv.at[k, slot], r, zs[k]).wait_recv()
            total = total + z_in[k, slot]
        esum[slot] = total
        i, j = PAIRS[n]
        if i > 0:
            direct_copy(n).start()
        if i != j:
            for half in range(2):
                mirror_copy(n, half).start()

    def drain_early(n):
        i, j = PAIRS[n]
        if i > 0:
            direct_copy(n).wait_send()
        if i != j:
            for half in range(2):
                mirror_copy(n, half).wait_send()

    def strip_product(s):
        a, b = strips[s]
        m = b - a
        h = jnp.concatenate([hi[far, a:b], hi[far, block + a:block + b]], axis=0)
        both = jnp.concatenate([h, lo[far, a:b], lo[far, block + a:block + b]], axis=0)
        for j in range(chips):
            value = dot_t(both, hi[j])
            value = value[:2 * m] + value[2 * m:] + dot_t(h, lo[j])
            lpart[j, 0, a:b] = value[:m]
            lpart[j, 1, a:b] = value[m:]

    def late_pair(s):
        a, b = strips[s]
        rng = pl.ds(a, b - a)
        return remote(lpart.at[:, 1, rng], lpair.at[:, rng], lp_send.at[s], lp_recv.at[s], mate[1], z)

    def late_z(s, k):
        a, b = strips[s]
        rng = pl.ds(a, b - a)
        return remote(
            lsum.at[differ(mine, k, zbits), rng], lz_in.at[k, rng], lz_send.at[k, s], lz_recv.at[k, s], r, zs[k]
        )

    def late_direct(s):
        a, b = strips[s]
        rng = pl.ds(a, b - a)
        return remote(lout.at[rng], ld_in.at[rng], ld_send.at[s], ld_recv.at[s], row_of(near[far], 0), z)

    def late_mirror(s, half):
        a, b = strips[s]
        rng = pl.ds(a, b - a)
        return remote(
            lout.at[rng, pl.ds(half * block, block)], lm_in.at[half, rng],
            lm_send.at[half, s], lm_recv.at[half, s], row_of(z, half), near[far],
        )

    def late_finish(s):
        a, b = strips[s]
        late_pair(s).wait_recv()
        for j in range(chips):
            lsum[j, a:b] = joined(lpart[j, 0, a:b], lpair[j, a:b])
        for k in range(cols - 1, 0, -1):
            late_z(s, k).start()

    def late_gather(s):
        a, b = strips[s]
        total = lsum[mine, a:b]
        for k in range(1, cols):
            late_z(s, k).wait_recv()
            total = total + lz_in[k, a:b]
        lout[a:b] = total
        for half in range(2):
            late_mirror(s, half).start()
        late_direct(s).start()

    own.wait()
    split(0, 0, block)
    whole(1).wait_recv()
    split(1, 0, block)
    product(0)
    finish(0)
    for k in early[1:far]:
        whole(k).wait_send()
    for s in range(2):
        for h in range(2):
            strip_copy(h, s).start()
    for g in range(1, far):
        for k in (2 * g, 2 * g + 1):
            whole(k).wait_recv()
            split(k, 0, block)
        fresh = [n for n, pair in enumerate(PAIRS) if pair[0] == g]
        for n in fresh:
            product(n)
        for n in fresh:
            finish(n)

    for s, (a, b) in enumerate(strips):
        for h in range(2):
            strip_copy(h, s).wait_recv()
        if s + 2 < len(strips):
            for h in range(2):
                strip_copy(h, s).wait_send()
            for h in range(2):
                strip_copy(h, s + 2).start()
        for h in range(2):
            split(2 * far + h, a, b)
        strip_product(s)
        late_pair(s).start()
        late_finish(s)
        if s > 0:
            late_gather(s - 1)
        if s == len(strips) - 3:
            each_early(gather_early)
    late_gather(len(strips) - 1)

    remote(esum.at[0], ed_in.at[0], e_send.at[0], e_recv.at[0], mate[1], z).wait_recv()

    @pl.when(mine == 0)
    def _():
        remote(esum.at[0], ed_in.at[1], e_send.at[0], e_recv.at[1], mate[1], z).wait_recv()
        work[...] = esum[0] + ed_in[0] + ed_in[1]

    @pl.when(mine != 0)
    def _():
        for half in range(2):
            remote(
                esum.at[0, :, pl.ds(half * block, block)], em_in.at[half], em_send.at[0, half], em_recv.at[half], mate[1], z
            ).wait_recv()
            at = slice(half * block, (half + 1) * block)
            work[:, at] = ed_in[0, :, at] + em_in[half].T

    for s in range(len(strips)):
        late_direct(s).wait_recv()
        for half in range(2):
            late_mirror(s, half).wait_recv()
    row = lax.broadcasted_iota(jnp.int32, (block, block), 0)
    column = lax.broadcasted_iota(jnp.int32, (block, block), 1)
    start = jnp.zeros((block, block), jnp.int32)
    for a, b in strips:
        start = jnp.where(column >= a, a, start)
    keep = jnp.logical_or(row < start, mine != 0)
    for half in range(2):
        at = slice(half * block, (half + 1) * block)
        mirrored = jnp.where(keep, lm_in[half].T, 0.0)
        total = (work[:, at] + ld_in[:, at] + mirrored) * scale
        to = core * block if half == 0 else (1 - core) * block
        gram[:, pl.ds(pl.multiple_of(to, block), block)] = total

    gram_copy = remote(gram, gmate, g_sem.at[0], g_sem.at[1], mate[1], z)
    gram_copy.start()

    def projection(left, right):
        return lax.dot_general(
            left, right, (((0,), (0,)), ((), ())),
            precision=lax.Precision.HIGHEST, preferred_element_type=jnp.float32,
        )

    def term_copy(i):
        return remote(term.at[near[i]], term_in.at[i], t_send.at[i], t_recv.at[i], row_of(near[i], 0), z)

    value = projection(fown[...], gram[...])
    factor_copy.wait_recv()
    gram_copy.wait_recv()
    value = value + projection(fmate[...], gmate[...])
    for i in range(chips):
        term[i] = value[i * share:(i + 1) * share]
    for i in range(chips - 1, 0, -1):
        term_copy(i).start()
    total = term[chip]
    for i in range(1, chips):
        term_copy(i).wait_recv()
        total = total + term_in[i]
    proj[...] = total

    for k in [1] + early[far:]:
        whole(k).wait_send()
    factor_copy.wait_send()
    gram_copy.wait_send()
    for i in range(1, chips):
        term_copy(i).wait_send()
    for n in range(len(PAIRS)):
        pair_copy(n).wait_send()
        plane, copy = z_copy(n)

        @pl.when(plane != z)
        def _():
            copy.wait_send()
    each_early(drain_early)
    for s in range(len(strips)):
        if s + 2 >= len(strips):
            for h in range(2):
                strip_copy(h, s).wait_send()
        late_pair(s).wait_send()
        for k in range(1, cols):
            late_z(s, k).wait_send()
        late_direct(s).wait_send()
        for half in range(2):
            late_mirror(s, half).wait_send()


def hand_on(gram, proj, gram_out, proj_out):
    gram_out[...] = gram[...]
    proj_out[...] = proj[...]


def fused(pixels, factor):
    rows, cols = lax.axis_size("row"), lax.axis_size("col")
    views, colours, block, depth = pixels.shape
    count = views * colours
    per = count // rows
    chips = rows // 2
    rank = factor.shape[1]
    scale = 1.0 / (count * depth * cols)
    unit = block // 8
    cuts = (0, 4 * unit, 6 * unit, 7 * unit, block)
    n = len(cuts) - 1
    pairs = len(PAIRS)
    vmem, dma = pltpu.VMEM, pltpu.SemaphoreType.DMA
    f32 = jnp.float32
    in_vmem = pl.BlockSpec(memory_space=pltpu.VMEM)
    shapes = (
        jax.ShapeDtypeStruct((block, 2 * block), f32),
        jax.ShapeDtypeStruct((rank // rows, 2 * block), f32),
    )
    gram, proj = pl.pallas_call(
        functools.partial(kernel, rows, cols, scale, cuts),
        out_shape=shapes,
        in_specs=[pl.BlockSpec(memory_space=pl.ANY), in_vmem],
        out_specs=(in_vmem, in_vmem),
        scratch_shapes=[
            vmem((rows, per, block, depth), f32),
            vmem((chips, 2 * block, per * depth), jnp.bfloat16),
            vmem((chips, 2 * block, per * depth), jnp.bfloat16),
            vmem((pairs, 2, block, 2 * block), f32),
            vmem((pairs, block, 2 * block), f32),
            vmem((pairs, block, 2 * block), f32),
            vmem((cols, SLOTS, block, 2 * block), f32),
            vmem((SLOTS, block, 2 * block), f32),
            vmem((2, block, 2 * block), f32),
            vmem((2, block, block), f32),
            vmem((chips, 2, block, 2 * block), f32),
            vmem((chips, block, 2 * block), f32),
            vmem((chips, block, 2 * block), f32),
            vmem((cols, block, 2 * block), f32),
            vmem((block, 2 * block), f32),
            vmem((block, 2 * block), f32),
            vmem((2, block, block), f32),
            vmem((block, 2 * block), f32),
            vmem((block, rank // 2), f32),
            vmem((block, rank // 2), f32),
            vmem((block, rank // 2), f32),
            vmem((block, 2 * block), f32),
            vmem((chips, rank // rows, 2 * block), f32),
            vmem((chips, rank // rows, 2 * block), f32),
            dma,
            dma((rows,)), dma((rows,)),
            dma((2, n)), dma((2, n)),
            dma((pairs,)), dma((pairs,)),
            dma((pairs,)), dma((cols, SLOTS)),
            dma((SLOTS,)), dma((2,)),
            dma((SLOTS, 2)), dma((2,)),
            dma((n,)), dma((n,)),
            dma((cols, n)), dma((cols, n)),
            dma((n,)), dma((n,)),
            dma((2, n)), dma((2, n)),
            dma((2,)), dma((2,)),
            dma((chips,)), dma((chips,)),
        ],
        compiler_params=pltpu.CompilerParams(
            collective_id=0, has_side_effects=True, vmem_limit_bytes=56 * 1024 * 1024
        ),
    )(pixels.reshape(count, block, depth), factor)
    gram, proj = pl.pallas_call(hand_on, out_shape=shapes, in_specs=[in_vmem] * 2, out_specs=(in_vmem, in_vmem))(gram, proj)
    return gram, proj.T


def pair_rows(own, others):
    return jnp.einsum(
        "vciw,vcjw->ij", own, others, precision=lax.Precision.HIGHEST, preferred_element_type=jnp.float32
    )


def general(pixels, factor):
    col_count = lax.axis_size("col")
    row_count = lax.axis_size("row")
    weight_scale = 1.0 / (pixels.shape[0] * pixels.shape[1] * pixels.shape[3] * col_count)
    row_block = pixels.shape[2]
    slices = lax.all_to_all(pixels, "row", split_axis=3, concat_axis=2, tiled=True)
    partial_value = pair_rows(slices, slices) * weight_scale
    width = partial_value.shape[0] // col_count
    arranged = partial_value.reshape(row_count, row_block, col_count, width)
    arranged = jnp.transpose(arranged, (0, 2, 1, 3)).reshape(row_count * col_count * row_block, width)
    block = lax.psum_scatter(arranged, ("row", "col"), scatter_dimension=0, tiled=True)
    term = lax.dot_general(
        block, factor, (((0,), (0,)), ((), ())),
        precision=lax.Precision.HIGHEST, preferred_element_type=jnp.float32,
    )
    summed_term = lax.psum(term, "row")
    share = summed_term.shape[1] // row_count
    projected = lax.dynamic_slice_in_dim(summed_term, lax.axis_index("row") * share, share, 1)
    return (block, projected)


def shards(pixels, factor):
    rows, cols = lax.axis_size("row"), lax.axis_size("col")
    views, colours, block, depth = pixels.shape
    fits = (
        rows == 2 * cols
        and cols == len({t for t, _ in EARLY.values()})
        and (views * colours) % rows == 0
        and block % 128 == 0
        and depth % 128 == 0
        and factor.shape[1] % (8 * rows) == 0
        and 8 * rows * block * (views * colours // rows) * depth <= 16 * 1024 * 1024
    )
    return (fused if fits else general)(pixels, factor)


def solution(mesh):
    in_specs = (P(None, None, "row", "col"), P("row", None))
    out_specs = (P("row", "col"), P("col", "row"))
    return jax.shard_map(shards, mesh=mesh, in_specs=in_specs, out_specs=out_specs, check_vma=False)
```

```python
import functools

import jax
import jax.numpy as jnp
from jax import lax
from jax.experimental import pallas as pl
from jax.experimental.pallas import tpu as pltpu
from jax.sharding import PartitionSpec as P

MESH = pl.DeviceIdType.MESH

EARLY = {(0, 0): (0, 0), (1, 0): (0, 1), (1, 1): (1, 0), (2, 0): (0, 2), (2, 1): (3, 0), (2, 2): (2, 0)}
PAIRS = list(EARLY)
SLOTS = 3


def flip(value, mask, bits):
    out = 0
    for b in range(bits):
        bit = (value // (1 << b)) % 2
        out = out + (1 << b) * ((1 - bit) if (mask >> b) & 1 else bit)
    return out


def differ(left, right, bits):
    out = 0
    for b in range(bits):
        out = out + (1 << b) * (((left // (1 << b)) + (right // (1 << b))) % 2)
    return out


def dot_t(a, b):
    return lax.dot_general(a, b, (((1,), (1,)), ((), ())), preferred_element_type=jnp.float32)


def kernel(
    rows, cols, scale, cuts,
    pix, fac, gram, proj,
    xs, hi, lo, part, pair_in, summed, z_in, esum, ed_in, em_in,
    lpart, lpair, lsum, lz_in, lout, ld_in, lm_in, work, fown, fout, fmate, gmate, term, term_in,
    own_sem, a_send, a_recv, d_send, d_recv, p_send, p_recv, z_send, z_recv, e_send, e_recv, em_send, em_recv,
    lp_send, lp_recv, lz_send, lz_recv, ld_send, ld_recv, lm_send, lm_recv, f_sem, g_send, g_recv, t_send, t_recv,
):
    r = lax.axis_index("row")
    z = lax.axis_index("col")
    core = r % 2
    chip = r // 2
    rbits = rows.bit_length() - 1
    zbits = cols.bit_length() - 1
    chips = rows // 2
    far = chips - 1
    mine = differ(chip, z, zbits)
    per = pix.shape[0] // rows
    block = pix.shape[1]
    depth = pix.shape[2]
    mate = [flip(r, k, rbits) for k in range(rows)]
    zs = [flip(z, k, zbits) for k in range(cols)]
    near = [flip(chip, i, zbits) for i in range(chips)]
    strips = list(zip(cuts[:-1], cuts[1:]))

    def remote(src, dst, send, recv, row, plane):
        return pltpu.make_async_remote_copy(
            src_ref=src, dst_ref=dst, send_sem=send, recv_sem=recv, device_id=(row, plane), device_id_type=MESH
        )

    barrier = pltpu.get_barrier_semaphore()
    for k in range(rows):
        for kz in range(cols):
            if (k == 0) != (kz == 0):
                pl.semaphore_signal(barrier, inc=1, device_id=(mate[k], zs[kz]), device_id_type=MESH)
    own = pltpu.make_async_copy(pix.at[pl.ds(r * per, per)], xs.at[0], own_sem)
    own.start()
    hi[far] = jnp.zeros(hi.shape[1:], hi.dtype)
    lo[far] = jnp.zeros(lo.shape[1:], lo.dtype)
    pl.semaphore_wait(barrier, rows + cols - 2)

    def whole(k):
        return remote(pix.at[pl.ds(mate[k] * per, per)], xs.at[k], a_send.at[k], a_recv.at[k], mate[k], z)

    def strip_copy(h, s):
        a, b = strips[s]
        k = 2 * far + h
        return remote(
            pix.at[pl.ds(mate[k] * per, per), pl.ds(a, b - a)], xs.at[k, :, pl.ds(a, b - a)],
            d_send.at[h, s], d_recv.at[h, s], mate[k], z,
        )

    share = fac.shape[1] // rows
    for i in range(chips):
        even = fac[:, 2 * i * share:(2 * i + 1) * share]
        odd = fac[:, (2 * i + 1) * share:(2 * i + 2) * share]
        fown[:, i * share:(i + 1) * share] = jnp.where(core == 0, even, odd)
        fout[:, i * share:(i + 1) * share] = jnp.where(core == 0, odd, even)

    early = [1] + list(range(2, 2 * far, 2)) + list(range(3, 2 * far, 2))
    for k in early:
        whole(k).start()
    factor_copy = remote(fout, fmate, f_sem.at[0], f_sem.at[1], mate[1], z)
    factor_copy.start()

    def split(k, a, b):
        at = k % 2 * block
        for p in range(per):
            x = xs[k, p, a:b]
            h = x.astype(jnp.bfloat16)
            hi[k // 2, at + a:at + b, p * depth:(p + 1) * depth] = h
            lo[k // 2, at + a:at + b, p * depth:(p + 1) * depth] = (x - h.astype(jnp.float32)).astype(jnp.bfloat16)

    def joined(left, right):
        other = jnp.concatenate([right[:, block:], right[:, :block]], axis=1)
        return left + other

    def pair_copy(n):
        return remote(part.at[n, 1], pair_in.at[n], p_send.at[n], p_recv.at[n], mate[1], z)

    def z_copy(n):
        t, slot = EARLY[PAIRS[n]]
        k = differ(z, near[t], zbits)
        return near[t], remote(summed.at[n], z_in.at[k, slot], z_send.at[n], z_recv.at[k, slot], r, near[t])

    def product(n):
        i, j = PAIRS[n]
        value = dot_t(hi[i], hi[j]) + dot_t(hi[i], lo[j]) + dot_t(lo[i], hi[j])
        part[n, 0] = value[:block]
        part[n, 1] = value[block:]
        pair_copy(n).start()

    def finish(n):
        pair_copy(n).wait_recv()
        summed[n] = joined(part[n, 0], pair_in[n])
        plane, copy = z_copy(n)

        @pl.when(plane != z)
        def _():
            copy.start()

    def row_of(chip_at, half):
        return 2 * chip_at + (core if half == 0 else 1 - core)

    def direct_copy(n):
        i, j = PAIRS[n]
        slot = EARLY[PAIRS[n]][1]
        to = 1 if (i, j) == (2, 2) else 0
        return remote(esum.at[slot], ed_in.at[to], e_send.at[slot], e_recv.at[to], row_of(near[i], 0), near[j])

    def mirror_copy(n, half):
        i, j = PAIRS[n]
        slot = EARLY[PAIRS[n]][1]
        return remote(
            esum.at[slot, :, pl.ds(half * block, block)], em_in.at[half],
            em_send.at[slot, half], em_recv.at[half], row_of(near[j], half), near[i],
        )

    def each_early(action):
        for t in range(chips):
            @pl.when(mine == t)
            def _():
                for n, pair in enumerate(PAIRS):
                    if EARLY[pair][0] == t:
                        action(n)

    def gather_early(n):
        slot = EARLY[PAIRS[n]][1]
        total = summed[n]
        for k in range(1, cols):
            remote(summed.at[n], z_in.at[k, slot], z_send.at[n], z_recv.at[k, slot], r, zs[k]).wait_recv()
            total = total + z_in[k, slot]
        esum[slot] = total
        i, j = PAIRS[n]
        if i > 0:
            direct_copy(n).start()
        if i != j:
            for half in range(2):
                mirror_copy(n, half).start()

    def drain_early(n):
        i, j = PAIRS[n]
        if i > 0:
            direct_copy(n).wait_send()
        if i != j:
            for half in range(2):
                mirror_copy(n, half).wait_send()

    def strip_product(s):
        a, b = strips[s]
        m = b - a
        h = jnp.concatenate([hi[far, a:b], hi[far, block + a:block + b]], axis=0)
        both = jnp.concatenate([h, lo[far, a:b], lo[far, block + a:block + b]], axis=0)
        for j in range(chips):
            value = dot_t(both, hi[j])
            value = value[:2 * m] + value[2 * m:] + dot_t(h, lo[j])
            lpart[j, 0, a:b] = value[:m]
            lpart[j, 1, a:b] = value[m:]

    def late_pair(s):
        a, b = strips[s]
        rng = pl.ds(a, b - a)
        return remote(lpart.at[:, 1, rng], lpair.at[:, rng], lp_send.at[s], lp_recv.at[s], mate[1], z)

    def late_z(s, k):
        a, b = strips[s]
        rng = pl.ds(a, b - a)
        return remote(
            lsum.at[differ(mine, k, zbits), rng], lz_in.at[k, rng], lz_send.at[k, s], lz_recv.at[k, s], r, zs[k]
        )

    def late_direct(s):
        a, b = strips[s]
        rng = pl.ds(a, b - a)
        return remote(lout.at[rng], ld_in.at[rng], ld_send.at[s], ld_recv.at[s], row_of(near[far], 0), z)

    def late_mirror(s, half):
        a, b = strips[s]
        rng = pl.ds(a, b - a)
        return remote(
            lout.at[rng, pl.ds(half * block, block)], lm_in.at[half, rng],
            lm_send.at[half, s], lm_recv.at[half, s], row_of(z, half), near[far],
        )

    def late_finish(s):
        a, b = strips[s]
        late_pair(s).wait_recv()
        for j in range(chips):
            lsum[j, a:b] = joined(lpart[j, 0, a:b], lpair[j, a:b])
        for k in range(cols - 1, 0, -1):
            late_z(s, k).start()

    def late_gather(s):
        a, b = strips[s]
        total = lsum[mine, a:b]
        for k in range(1, cols):
            late_z(s, k).wait_recv()
            total = total + lz_in[k, a:b]
        lout[a:b] = total
        for half in range(2):
            late_mirror(s, half).start()
        late_direct(s).start()

    own.wait()
    split(0, 0, block)
    whole(1).wait_recv()
    split(1, 0, block)
    product(0)
    finish(0)
    for k in early[1:far]:
        whole(k).wait_send()
    for s in range(2):
        for h in range(2):
            strip_copy(h, s).start()
    for g in range(1, far):
        for k in (2 * g, 2 * g + 1):
            whole(k).wait_recv()
            split(k, 0, block)
        fresh = [n for n, pair in enumerate(PAIRS) if pair[0] == g]
        for n in fresh:
            product(n)
        for n in fresh:
            finish(n)

    for s, (a, b) in enumerate(strips):
        for h in range(2):
            strip_copy(h, s).wait_recv()
        if s + 2 < len(strips):
            for h in range(2):
                strip_copy(h, s).wait_send()
            for h in range(2):
                strip_copy(h, s + 2).start()
        for h in range(2):
            split(2 * far + h, a, b)
        strip_product(s)
        late_pair(s).start()
        late_finish(s)
        if s > 0:
            late_gather(s - 1)
        if s == len(strips) - 3:
            each_early(gather_early)
    late_gather(len(strips) - 1)

    remote(esum.at[0], ed_in.at[0], e_send.at[0], e_recv.at[0], mate[1], z).wait_recv()

    @pl.when(mine == 0)
    def _():
        remote(esum.at[0], ed_in.at[1], e_send.at[0], e_recv.at[1], mate[1], z).wait_recv()
        work[...] = esum[0] + ed_in[0] + ed_in[1]

    @pl.when(mine != 0)
    def _():
        for half in range(2):
            remote(
                esum.at[0, :, pl.ds(half * block, block)], em_in.at[half], em_send.at[0, half], em_recv.at[half], mate[1], z
            ).wait_recv()
            at = slice(half * block, (half + 1) * block)
            work[:, at] = ed_in[0, :, at] + em_in[half].T

    row = lax.broadcasted_iota(jnp.int32, (block, block), 0)
    column = lax.broadcasted_iota(jnp.int32, (block, block), 1)
    start = jnp.zeros((block, block), jnp.int32)
    for a, b in strips:
        start = jnp.where(column >= a, a, start)
    keep = jnp.logical_or(row < start, mine != 0)

    def late_arrive(s):
        late_direct(s).wait_recv()
        for half in range(2):
            late_mirror(s, half).wait_recv()

    def late_terms(half, a, b):
        at = slice(half * block, (half + 1) * block)
        above, below = jnp.zeros((a, block), jnp.float32), jnp.zeros((block - b, block), jnp.float32)
        whole_of = lambda x: jnp.concatenate([v for v in (above, x, below) if v.shape[0]], axis=0)
        return at, whole_of(ld_in[a:b, at]) + jnp.where(keep, whole_of(lm_in[half, a:b]).T, 0.0)

    a, b = strips[-1]
    for s in range(len(strips) - 1):
        late_arrive(s)
    for half in range(2):
        at, terms = late_terms(half, 0, a)
        work[:, at] = work[:, at] + terms
    late_arrive(len(strips) - 1)

    def gram_copy(half):
        to = core * block if half == 0 else (1 - core) * block
        at = pl.ds(pl.multiple_of(to, block), block)
        return at, remote(gram.at[:, at], gmate.at[:, at], g_send.at[half], g_recv.at[half], mate[1], z)

    for half in range(2):
        at, terms = late_terms(half, a, b)
        to, copy = gram_copy(half)
        gram[:, to] = (work[:, at] + terms) * scale
        copy.start()

    def projection(left, right):
        return lax.dot_general(
            left, right, (((0,), (0,)), ((), ())),
            precision=lax.Precision.HIGHEST, preferred_element_type=jnp.float32,
        )

    def term_copy(i):
        return remote(term.at[near[i]], term_in.at[i], t_send.at[i], t_recv.at[i], row_of(near[i], 0), z)

    value = projection(fown[...], gram[...])
    factor_copy.wait_recv()
    for half in range(2):
        at = pl.ds(pl.multiple_of((1 - core) * block if half == 0 else core * block, block), block)
        remote(gram.at[:, at], gmate.at[:, at], g_send.at[half], g_recv.at[half], mate[1], z).wait_recv()
    value = value + projection(fmate[...], gmate[...])
    for i in range(chips):
        term[i] = value[i * share:(i + 1) * share]
    for i in range(chips - 1, 0, -1):
        term_copy(i).start()
    total = term[chip]
    for i in range(1, chips):
        term_copy(i).wait_recv()
        total = total + term_in[i]
    proj[...] = total

    for k in [1] + early[far:]:
        whole(k).wait_send()
    factor_copy.wait_send()
    for half in range(2):
        gram_copy(half)[1].wait_send()
    for i in range(1, chips):
        term_copy(i).wait_send()
    for n in range(len(PAIRS)):
        pair_copy(n).wait_send()
        plane, copy = z_copy(n)

        @pl.when(plane != z)
        def _():
            copy.wait_send()
    each_early(drain_early)
    for s in range(len(strips)):
        if s + 2 >= len(strips):
            for h in range(2):
                strip_copy(h, s).wait_send()
        late_pair(s).wait_send()
        for k in range(1, cols):
            late_z(s, k).wait_send()
        late_direct(s).wait_send()
        for half in range(2):
            late_mirror(s, half).wait_send()


def hand_on(gram, proj, gram_out, proj_out):
    gram_out[...] = gram[...]
    proj_out[...] = proj[...]


def fused(pixels, factor):
    rows, cols = lax.axis_size("row"), lax.axis_size("col")
    views, colours, block, depth = pixels.shape
    count = views * colours
    per = count // rows
    chips = rows // 2
    rank = factor.shape[1]
    scale = 1.0 / (count * depth * cols)
    unit = block // 8
    cuts = (0, 4 * unit, 6 * unit, 7 * unit, block)
    n = len(cuts) - 1
    pairs = len(PAIRS)
    vmem, dma = pltpu.VMEM, pltpu.SemaphoreType.DMA
    f32 = jnp.float32
    in_vmem = pl.BlockSpec(memory_space=pltpu.VMEM)
    shapes = (
        jax.ShapeDtypeStruct((block, 2 * block), f32),
        jax.ShapeDtypeStruct((rank // rows, 2 * block), f32),
    )
    gram, proj = pl.pallas_call(
        functools.partial(kernel, rows, cols, scale, cuts),
        out_shape=shapes,
        in_specs=[pl.BlockSpec(memory_space=pl.ANY), in_vmem],
        out_specs=(in_vmem, in_vmem),
        scratch_shapes=[
            vmem((rows, per, block, depth), f32),
            vmem((chips, 2 * block, per * depth), jnp.bfloat16),
            vmem((chips, 2 * block, per * depth), jnp.bfloat16),
            vmem((pairs, 2, block, 2 * block), f32),
            vmem((pairs, block, 2 * block), f32),
            vmem((pairs, block, 2 * block), f32),
            vmem((cols, SLOTS, block, 2 * block), f32),
            vmem((SLOTS, block, 2 * block), f32),
            vmem((2, block, 2 * block), f32),
            vmem((2, block, block), f32),
            vmem((chips, 2, block, 2 * block), f32),
            vmem((chips, block, 2 * block), f32),
            vmem((chips, block, 2 * block), f32),
            vmem((cols, block, 2 * block), f32),
            vmem((block, 2 * block), f32),
            vmem((block, 2 * block), f32),
            vmem((2, block, block), f32),
            vmem((block, 2 * block), f32),
            vmem((block, rank // 2), f32),
            vmem((block, rank // 2), f32),
            vmem((block, rank // 2), f32),
            vmem((block, 2 * block), f32),
            vmem((chips, rank // rows, 2 * block), f32),
            vmem((chips, rank // rows, 2 * block), f32),
            dma,
            dma((rows,)), dma((rows,)),
            dma((2, n)), dma((2, n)),
            dma((pairs,)), dma((pairs,)),
            dma((pairs,)), dma((cols, SLOTS)),
            dma((SLOTS,)), dma((2,)),
            dma((SLOTS, 2)), dma((2,)),
            dma((n,)), dma((n,)),
            dma((cols, n)), dma((cols, n)),
            dma((n,)), dma((n,)),
            dma((2, n)), dma((2, n)),
            dma((2,)), dma((2,)), dma((2,)),
            dma((chips,)), dma((chips,)),
        ],
        compiler_params=pltpu.CompilerParams(
            collective_id=0, has_side_effects=True, vmem_limit_bytes=56 * 1024 * 1024
        ),
    )(pixels.reshape(count, block, depth), factor)
    gram, proj = pl.pallas_call(hand_on, out_shape=shapes, in_specs=[in_vmem] * 2, out_specs=(in_vmem, in_vmem))(gram, proj)
    return gram, proj.T


def pair_rows(own, others):
    return jnp.einsum(
        "vciw,vcjw->ij", own, others, precision=lax.Precision.HIGHEST, preferred_element_type=jnp.float32
    )


def general(pixels, factor):
    col_count = lax.axis_size("col")
    row_count = lax.axis_size("row")
    weight_scale = 1.0 / (pixels.shape[0] * pixels.shape[1] * pixels.shape[3] * col_count)
    row_block = pixels.shape[2]
    slices = lax.all_to_all(pixels, "row", split_axis=3, concat_axis=2, tiled=True)
    partial_value = pair_rows(slices, slices) * weight_scale
    width = partial_value.shape[0] // col_count
    arranged = partial_value.reshape(row_count, row_block, col_count, width)
    arranged = jnp.transpose(arranged, (0, 2, 1, 3)).reshape(row_count * col_count * row_block, width)
    block = lax.psum_scatter(arranged, ("row", "col"), scatter_dimension=0, tiled=True)
    term = lax.dot_general(
        block, factor, (((0,), (0,)), ((), ())),
        precision=lax.Precision.HIGHEST, preferred_element_type=jnp.float32,
    )
    summed_term = lax.psum(term, "row")
    share = summed_term.shape[1] // row_count
    projected = lax.dynamic_slice_in_dim(summed_term, lax.axis_index("row") * share, share, 1)
    return (block, projected)


def shards(pixels, factor):
    rows, cols = lax.axis_size("row"), lax.axis_size("col")
    views, colours, block, depth = pixels.shape
    fits = (
        rows == 2 * cols
        and cols == len({t for t, _ in EARLY.values()})
        and (views * colours) % rows == 0
        and block % 128 == 0
        and depth % 128 == 0
        and factor.shape[1] % (8 * rows) == 0
        and 8 * rows * block * (views * colours // rows) * depth <= 16 * 1024 * 1024
    )
    return (fused if fits else general)(pixels, factor)


def solution(mesh):
    in_specs = (P(None, None, "row", "col"), P("row", None))
    out_specs = (P("row", "col"), P("col", "row"))
    return jax.shard_map(shards, mesh=mesh, in_specs=in_specs, out_specs=out_specs, check_vma=False)
```

```python
import functools

import jax
import jax.numpy as jnp
from jax import lax
from jax.experimental import pallas as pl
from jax.experimental.pallas import tpu as pltpu
from jax.sharding import PartitionSpec as P

MESH = pl.DeviceIdType.MESH

EARLY = {(0, 0): (0, 0), (1, 0): (0, 1), (1, 1): (1, 0), (2, 0): (1, 1), (2, 1): (3, 0), (2, 2): (2, 0)}
PAIRS = list(EARLY)
SLOTS = 2


def flip(value, mask, bits):
    out = 0
    for b in range(bits):
        bit = (value // (1 << b)) % 2
        out = out + (1 << b) * ((1 - bit) if (mask >> b) & 1 else bit)
    return out


def differ(left, right, bits):
    out = 0
    for b in range(bits):
        out = out + (1 << b) * (((left // (1 << b)) + (right // (1 << b))) % 2)
    return out


def dot_t(a, b):
    return lax.dot_general(a, b, (((1,), (1,)), ((), ())), preferred_element_type=jnp.float32)


def kernel(
    rows, cols, scale, cuts,
    pix, fac, gram, proj,
    xs, hi, lo, part, pair_in, summed, z_in, esum, ed_in, em_in,
    lpart, lpair, lsum, lz_in, lout, ld_in, lm_in, work, fown, fout, fmate, gmate, term, term_in,
    own_sem, a_send, a_recv, d_send, d_recv, p_send, p_recv, z_send, z_recv, e_send, e_recv, em_send, em_recv,
    lp_send, lp_recv, lz_send, lz_recv, ld_send, ld_recv, lm_send, lm_recv, f_sem, g_sem, t_send, t_recv,
):
    r = lax.axis_index("row")
    z = lax.axis_index("col")
    core = r % 2
    chip = r // 2
    rbits = rows.bit_length() - 1
    zbits = cols.bit_length() - 1
    chips = rows // 2
    far = chips - 1
    mine = differ(chip, z, zbits)
    per = pix.shape[0] // rows
    block = pix.shape[1]
    depth = pix.shape[2]
    mate = [flip(r, k, rbits) for k in range(rows)]
    zs = [flip(z, k, zbits) for k in range(cols)]
    near = [flip(chip, i, zbits) for i in range(chips)]
    strips = list(zip(cuts[:-1], cuts[1:]))

    def remote(src, dst, send, recv, row, plane):
        return pltpu.make_async_remote_copy(
            src_ref=src, dst_ref=dst, send_sem=send, recv_sem=recv, device_id=(row, plane), device_id_type=MESH
        )

    barrier = pltpu.get_barrier_semaphore()
    for k in range(rows):
        for kz in range(cols):
            if (k == 0) != (kz == 0):
                pl.semaphore_signal(barrier, inc=1, device_id=(mate[k], zs[kz]), device_id_type=MESH)
    own = pltpu.make_async_copy(pix.at[pl.ds(r * per, per)], xs.at[0], own_sem)
    own.start()
    hi[far] = jnp.zeros(hi.shape[1:], hi.dtype)
    lo[far] = jnp.zeros(lo.shape[1:], lo.dtype)
    pl.semaphore_wait(barrier, rows + cols - 2)

    def whole(k):
        return remote(pix.at[pl.ds(mate[k] * per, per)], xs.at[k], a_send.at[k], a_recv.at[k], mate[k], z)

    def strip_copy(h, s):
        a, b = strips[s]
        k = 2 * far + h
        return remote(
            pix.at[pl.ds(mate[k] * per, per), pl.ds(a, b - a)], xs.at[k, :, pl.ds(a, b - a)],
            d_send.at[h, s], d_recv.at[h, s], mate[k], z,
        )

    share = fac.shape[1] // rows
    for i in range(chips):
        even = fac[:, 2 * i * share:(2 * i + 1) * share]
        odd = fac[:, (2 * i + 1) * share:(2 * i + 2) * share]
        fown[:, i * share:(i + 1) * share] = jnp.where(core == 0, even, odd)
        fout[:, i * share:(i + 1) * share] = jnp.where(core == 0, odd, even)

    early = [1] + list(range(2, 2 * far, 2)) + list(range(3, 2 * far, 2))
    for k in early:
        whole(k).start()
    factor_copy = remote(fout, fmate, f_sem.at[0], f_sem.at[1], mate[1], z)
    factor_copy.start()

    def split(k, a, b):
        at = k % 2 * block
        for p in range(per):
            x = xs[k, p, a:b]
            h = x.astype(jnp.bfloat16)
            hi[k // 2, at + a:at + b, p * depth:(p + 1) * depth] = h
            lo[k // 2, at + a:at + b, p * depth:(p + 1) * depth] = (x - h.astype(jnp.float32)).astype(jnp.bfloat16)

    def joined(left, right):
        other = jnp.concatenate([right[:, block:], right[:, :block]], axis=1)
        return left + other

    def pair_copy(n):
        return remote(part.at[n, 1], pair_in.at[n], p_send.at[n], p_recv.at[n], mate[1], z)

    def z_copy(n):
        t, slot = EARLY[PAIRS[n]]
        k = differ(z, near[t], zbits)
        return near[t], remote(summed.at[n], z_in.at[k, slot], z_send.at[n], z_recv.at[k, slot], r, near[t])

    def product(n):
        i, j = PAIRS[n]
        value = dot_t(hi[i], hi[j]) + dot_t(hi[i], lo[j]) + dot_t(lo[i], hi[j])
        part[n, 0] = value[:block]
        part[n, 1] = value[block:]
        pair_copy(n).start()

    def finish(n):
        pair_copy(n).wait_recv()
        summed[n] = joined(part[n, 0], pair_in[n])
        plane, copy = z_copy(n)

        @pl.when(plane != z)
        def _():
            copy.start()

    def row_of(chip_at, half):
        return 2 * chip_at + (core if half == 0 else 1 - core)

    def direct_copy(n):
        i, j = PAIRS[n]
        slot = EARLY[PAIRS[n]][1]
        to = 1 if (i, j) == (2, 2) else 0
        return remote(esum.at[slot], ed_in.at[to], e_send.at[slot], e_recv.at[to], row_of(near[i], 0), near[j])

    def mirror_copy(n, half):
        i, j = PAIRS[n]
        slot = EARLY[PAIRS[n]][1]
        return remote(
            esum.at[slot, :, pl.ds(half * block, block)], em_in.at[half],
            em_send.at[slot, half], em_recv.at[half], row_of(near[j], half), near[i],
        )

    def each_early(action):
        for t in range(chips):
            @pl.when(mine == t)
            def _():
                for n, pair in enumerate(PAIRS):
                    if EARLY[pair][0] == t:
                        action(n)

    def gather_early(n):
        slot = EARLY[PAIRS[n]][1]
        total = summed[n]
        for k in range(1, cols):
            remote(summed.at[n], z_in.at[k, slot], z_send.at[n], z_recv.at[k, slot], r, zs[k]).wait_recv()
            total = total + z_in[k, slot]
        esum[slot] = total
        i, j = PAIRS[n]
        if i > 0:
            direct_copy(n).start()
        if i != j:
            for half in range(2):
                mirror_copy(n, half).start()

    def drain_early(n):
        i, j = PAIRS[n]
        if i > 0:
            direct_copy(n).wait_send()
        if i != j:
            for half in range(2):
                mirror_copy(n, half).wait_send()

    def strip_product(s):
        a, b = strips[s]
        m = b - a
        h = jnp.concatenate([hi[far, a:b], hi[far, block + a:block + b]], axis=0)
        both = jnp.concatenate([h, lo[far, a:b], lo[far, block + a:block + b]], axis=0)
        for j in range(chips):
            value = dot_t(both, hi[j])
            value = value[:2 * m] + value[2 * m:] + dot_t(h, lo[j])
            lpart[j, 0, a:b] = value[:m]
            lpart[j, 1, a:b] = value[m:]

    def late_pair(s):
        a, b = strips[s]
        rng = pl.ds(a, b - a)
        return remote(lpart.at[:, 1, rng], lpair.at[:, rng], lp_send.at[s], lp_recv.at[s], mate[1], z)

    def late_z(s, k):
        a, b = strips[s]
        rng = pl.ds(a, b - a)
        return remote(
            lsum.at[differ(mine, k, zbits), rng], lz_in.at[k, rng], lz_send.at[k, s], lz_recv.at[k, s], r, zs[k]
        )

    def late_direct(s):
        a, b = strips[s]
        rng = pl.ds(a, b - a)
        return remote(lout.at[rng], ld_in.at[rng], ld_send.at[s], ld_recv.at[s], row_of(near[far], 0), z)

    def late_mirror(s, half):
        a, b = strips[s]
        rng = pl.ds(a, b - a)
        return remote(
            lout.at[rng, pl.ds(half * block, block)], lm_in.at[half, rng],
            lm_send.at[half, s], lm_recv.at[half, s], row_of(z, half), near[far],
        )

    def late_finish(s):
        a, b = strips[s]
        late_pair(s).wait_recv()
        for j in range(chips):
            lsum[j, a:b] = joined(lpart[j, 0, a:b], lpair[j, a:b])
        for k in range(cols - 1, 0, -1):
            late_z(s, k).start()

    def late_gather(s):
        a, b = strips[s]
        total = lsum[mine, a:b]
        for k in range(1, cols):
            late_z(s, k).wait_recv()
            total = total + lz_in[k, a:b]
        lout[a:b] = total
        for half in range(2):
            late_mirror(s, half).start()
        late_direct(s).start()

    own.wait()
    split(0, 0, block)
    whole(1).wait_recv()
    split(1, 0, block)
    product(0)
    finish(0)
    for k in early[1:far]:
        whole(k).wait_send()
    for s in range(len(strips)):
        for h in range(2):
            strip_copy(h, s).start()
    for g in range(1, far):
        for k in (2 * g, 2 * g + 1):
            whole(k).wait_recv()
            split(k, 0, block)
        fresh = [n for n, pair in enumerate(PAIRS) if pair[0] == g]
        for n in fresh:
            product(n)
        for n in fresh:
            finish(n)

    for s, (a, b) in enumerate(strips):
        for h in range(2):
            strip_copy(h, s).wait_recv()
        for h in range(2):
            split(2 * far + h, a, b)
        strip_product(s)
        late_pair(s).start()
        late_finish(s)
        if s > 0:
            late_gather(s - 1)
        if s == len(strips) - 3:
            each_early(gather_early)
    late_gather(len(strips) - 1)

    remote(esum.at[0], ed_in.at[0], e_send.at[0], e_recv.at[0], mate[1], z).wait_recv()

    @pl.when(mine == 0)
    def _():
        remote(esum.at[0], ed_in.at[1], e_send.at[0], e_recv.at[1], mate[1], z).wait_recv()
        work[...] = esum[0] + ed_in[0] + ed_in[1]

    @pl.when(mine != 0)
    def _():
        for half in range(2):
            remote(
                esum.at[0, :, pl.ds(half * block, block)], em_in.at[half], em_send.at[0, half], em_recv.at[half], mate[1], z
            ).wait_recv()
            at = slice(half * block, (half + 1) * block)
            work[:, at] = ed_in[0, :, at] + em_in[half].T

    for s in range(len(strips)):
        late_direct(s).wait_recv()
        for half in range(2):
            late_mirror(s, half).wait_recv()
    row = lax.broadcasted_iota(jnp.int32, (block, block), 0)
    column = lax.broadcasted_iota(jnp.int32, (block, block), 1)
    start = jnp.zeros((block, block), jnp.int32)
    for a, b in strips:
        start = jnp.where(column >= a, a, start)
    keep = jnp.logical_or(row < start, mine != 0)
    for half in range(2):
        at = slice(half * block, (half + 1) * block)
        mirrored = jnp.where(keep, lm_in[half].T, 0.0)
        total = (work[:, at] + ld_in[:, at] + mirrored) * scale
        to = core * block if half == 0 else (1 - core) * block
        gram[:, pl.ds(pl.multiple_of(to, block), block)] = total

    gram_copy = remote(gram, gmate, g_sem.at[0], g_sem.at[1], mate[1], z)
    gram_copy.start()

    def projection(left, right):
        return lax.dot_general(
            left, right, (((0,), (0,)), ((), ())),
            precision=lax.Precision.HIGHEST, preferred_element_type=jnp.float32,
        )

    def term_copy(i):
        return remote(term.at[near[i]], term_in.at[i], t_send.at[i], t_recv.at[i], row_of(near[i], 0), z)

    value = projection(fown[...], gram[...])
    factor_copy.wait_recv()
    gram_copy.wait_recv()
    value = value + projection(fmate[...], gmate[...])
    for i in range(chips):
        term[i] = value[i * share:(i + 1) * share]
    for i in range(chips - 1, 0, -1):
        term_copy(i).start()
    total = term[chip]
    for i in range(1, chips):
        term_copy(i).wait_recv()
        total = total + term_in[i]
    proj[...] = total

    for k in [1] + early[far:]:
        whole(k).wait_send()
    factor_copy.wait_send()
    gram_copy.wait_send()
    for i in range(1, chips):
        term_copy(i).wait_send()
    for n in range(len(PAIRS)):
        pair_copy(n).wait_send()
        plane, copy = z_copy(n)

        @pl.when(plane != z)
        def _():
            copy.wait_send()
    each_early(drain_early)
    for s in range(len(strips)):
        for h in range(2):
            strip_copy(h, s).wait_send()
        late_pair(s).wait_send()
        for k in range(1, cols):
            late_z(s, k).wait_send()
        late_direct(s).wait_send()
        for half in range(2):
            late_mirror(s, half).wait_send()


def hand_on(gram, proj, gram_out, proj_out):
    gram_out[...] = gram[...]
    proj_out[...] = proj[...]


def fused(pixels, factor):
    rows, cols = lax.axis_size("row"), lax.axis_size("col")
    views, colours, block, depth = pixels.shape
    count = views * colours
    per = count // rows
    chips = rows // 2
    rank = factor.shape[1]
    scale = 1.0 / (count * depth * cols)
    unit = block // 8
    cuts = (0, 4 * unit, 6 * unit, 7 * unit, block)
    n = len(cuts) - 1
    pairs = len(PAIRS)
    vmem, dma = pltpu.VMEM, pltpu.SemaphoreType.DMA
    f32 = jnp.float32
    in_vmem = pl.BlockSpec(memory_space=pltpu.VMEM)
    shapes = (
        jax.ShapeDtypeStruct((block, 2 * block), f32),
        jax.ShapeDtypeStruct((rank // rows, 2 * block), f32),
    )
    gram, proj = pl.pallas_call(
        functools.partial(kernel, rows, cols, scale, cuts),
        out_shape=shapes,
        in_specs=[pl.BlockSpec(memory_space=pl.ANY), in_vmem],
        out_specs=(in_vmem, in_vmem),
        scratch_shapes=[
            vmem((rows, per, block, depth), f32),
            vmem((chips, 2 * block, per * depth), jnp.bfloat16),
            vmem((chips, 2 * block, per * depth), jnp.bfloat16),
            vmem((pairs, 2, block, 2 * block), f32),
            vmem((pairs, block, 2 * block), f32),
            vmem((pairs, block, 2 * block), f32),
            vmem((cols, SLOTS, block, 2 * block), f32),
            vmem((SLOTS, block, 2 * block), f32),
            vmem((2, block, 2 * block), f32),
            vmem((2, block, block), f32),
            vmem((chips, 2, block, 2 * block), f32),
            vmem((chips, block, 2 * block), f32),
            vmem((chips, block, 2 * block), f32),
            vmem((cols, block, 2 * block), f32),
            vmem((block, 2 * block), f32),
            vmem((block, 2 * block), f32),
            vmem((2, block, block), f32),
            vmem((block, 2 * block), f32),
            vmem((block, rank // 2), f32),
            vmem((block, rank // 2), f32),
            vmem((block, rank // 2), f32),
            vmem((block, 2 * block), f32),
            vmem((chips, rank // rows, 2 * block), f32),
            vmem((chips, rank // rows, 2 * block), f32),
            dma,
            dma((rows,)), dma((rows,)),
            dma((2, n)), dma((2, n)),
            dma((pairs,)), dma((pairs,)),
            dma((pairs,)), dma((cols, SLOTS)),
            dma((SLOTS,)), dma((2,)),
            dma((SLOTS, 2)), dma((2,)),
            dma((n,)), dma((n,)),
            dma((cols, n)), dma((cols, n)),
            dma((n,)), dma((n,)),
            dma((2, n)), dma((2, n)),
            dma((2,)), dma((2,)),
            dma((chips,)), dma((chips,)),
        ],
        compiler_params=pltpu.CompilerParams(
            collective_id=0, has_side_effects=True, vmem_limit_bytes=56 * 1024 * 1024
        ),
    )(pixels.reshape(count, block, depth), factor)
    gram, proj = pl.pallas_call(hand_on, out_shape=shapes, in_specs=[in_vmem] * 2, out_specs=(in_vmem, in_vmem))(gram, proj)
    return gram, proj.T


def pair_rows(own, others):
    return jnp.einsum(
        "vciw,vcjw->ij", own, others, precision=lax.Precision.HIGHEST, preferred_element_type=jnp.float32
    )


def general(pixels, factor):
    col_count = lax.axis_size("col")
    row_count = lax.axis_size("row")
    weight_scale = 1.0 / (pixels.shape[0] * pixels.shape[1] * pixels.shape[3] * col_count)
    row_block = pixels.shape[2]
    slices = lax.all_to_all(pixels, "row", split_axis=3, concat_axis=2, tiled=True)
    partial_value = pair_rows(slices, slices) * weight_scale
    width = partial_value.shape[0] // col_count
    arranged = partial_value.reshape(row_count, row_block, col_count, width)
    arranged = jnp.transpose(arranged, (0, 2, 1, 3)).reshape(row_count * col_count * row_block, width)
    block = lax.psum_scatter(arranged, ("row", "col"), scatter_dimension=0, tiled=True)
    term = lax.dot_general(
        block, factor, (((0,), (0,)), ((), ())),
        precision=lax.Precision.HIGHEST, preferred_element_type=jnp.float32,
    )
    summed_term = lax.psum(term, "row")
    share = summed_term.shape[1] // row_count
    projected = lax.dynamic_slice_in_dim(summed_term, lax.axis_index("row") * share, share, 1)
    return (block, projected)


def shards(pixels, factor):
    rows, cols = lax.axis_size("row"), lax.axis_size("col")
    views, colours, block, depth = pixels.shape
    fits = (
        rows == 2 * cols
        and cols == len({t for t, _ in EARLY.values()})
        and (views * colours) % rows == 0
        and block % 128 == 0
        and depth % 128 == 0
        and factor.shape[1] % (8 * rows) == 0
        and 8 * rows * block * (views * colours // rows) * depth <= 16 * 1024 * 1024
    )
    return (fused if fits else general)(pixels, factor)


def solution(mesh):
    in_specs = (P(None, None, "row", "col"), P("row", None))
    out_specs = (P("row", "col"), P("col", "row"))
    return jax.shard_map(shards, mesh=mesh, in_specs=in_specs, out_specs=out_specs, check_vma=False)
```
